32 devices in a mesh: panel: 8 (over y, x, core), rep: 4 (over z).
Axes of the slice: x: 2, y: 2, z: 4, core: 2. Of those that a mesh axis runs over, the one named last changes fastest.
Arguments:
- activations: float32 [98304, 1024], P(('panel', 'rep')), may hold values from 0 to 48
- out_grads: float32 [98304, 256], P(('panel', 'rep')), may hold values from -8 to 8
- factor_a: float32 [1024, 1024], P('panel'), may hold values from -7 to 27
- factor_g: float32 [256, 256], P('panel'), may hold values from -7 to 27
- inverse_a: float32 [1024, 1024], P('panel'), may hold values from -0.1875 to 0.1875
- inverse_g: float32 [256, 256], P('panel'), may hold values from -0.375 to 0.375
Outputs:
- new_factor_a: float32 [1024, 1024], P('panel')
- new_factor_g: float32 [256, 256], P('panel')
- precond_grad: float32 [1024, 256], P('panel')
The draws below stay inside these ranges and needn't reach their ends.
All inputs are finite; a program needn't handle non-finite values.
Results may differ from the reference program's by a relative error of at most 0.000076.
Values sent between devices are 32-bit elements; how exact they have to be, the bound alone decides.
A program may use at most 128 MiB of HBM per device.

```python
import math
import jax
import jax.numpy as jnp
from jax import lax

CIN = 1024
COUT = 256
ROWS_DEV = 3072
ROWS = 98304


def channel_scales(key):
    lower_log = math.log(0.3)
    upper_log = math.log(3.0)
    input_scale = jnp.exp(jax.random.uniform(jax.random.fold_in(key, 11), (CIN,), jnp.float32, lower_log, upper_log))
    output_scale = jnp.exp(jax.random.uniform(jax.random.fold_in(key, 12), (COUT,), jnp.float32, lower_log, upper_log))
    return (input_scale, output_scale)


def row_scales(key):
    return jnp.exp(jax.random.uniform(key, (ROWS, 1), jnp.float32, math.log(0.3), math.log(3.0)))


def draw_activations(key, part):
    input_scale, output_scale = channel_scales(key)
    base_key = jax.random.fold_in(key, 21)
    block_count = ROWS // ROWS_DEV
    row_scale = row_scales(jax.random.fold_in(base_key, 1))
    loading = jax.random.uniform(jax.random.fold_in(base_key, 2), (1, CIN), jnp.float32, 0.0, 1.0)
    shared_factor = jnp.clip(jax.random.normal(jax.random.fold_in(base_key, 3), (ROWS, 1), jnp.float32), -3.0, 3.0)
    block_means = jax.random.uniform(jax.random.fold_in(base_key, 4), (block_count, 1, CIN), jnp.float32, 0.2, 1.5)
    noise_part = jnp.clip(jax.random.normal(jax.random.fold_in(base_key, 5), (block_count, ROWS_DEV, CIN), jnp.float32), -3.0, 3.0)
    shrink_by = 1.0 / 1.5
    inner_sum = (block_means + noise_part).reshape(ROWS, CIN) + shared_factor * loading
    values = row_scale * input_scale[None, :] * jnp.maximum(inner_sum, 0.0) * shrink_by
    return values.astype(jnp.float32)


def draw_out_grads(key, part):
    input_scale, output_scale = channel_scales(key)
    base_key = jax.random.fold_in(key, 31)
    block_count = ROWS // ROWS_DEV
    row_scale = row_scales(jax.random.fold_in(base_key, 1))
    shared_factor = jnp.clip(jax.random.normal(jax.random.fold_in(base_key, 2), (ROWS, 1), jnp.float32), -3.0, 3.0)
    loading = jnp.clip(jax.random.normal(jax.random.fold_in(base_key, 3), (1, COUT), jnp.float32), -3.0, 3.0)
    block_dirs = jnp.clip(jax.random.normal(jax.random.fold_in(base_key, 4), (block_count, 1, COUT), jnp.float32), -3.0, 3.0)
    noise_part = jnp.clip(jax.random.normal(jax.random.fold_in(base_key, 5), (block_count, ROWS_DEV, COUT), jnp.float32), -3.0, 3.0)
    inner_sum = (0.7 * block_dirs + noise_part).reshape(ROWS, COUT) + shared_factor * loading
    values = row_scale * output_scale[None, :] * inner_sum / math.sqrt(ROWS)
    return values.astype(jnp.float32)


def symmetric_factor(key, scale_vector, order):
    entries = jnp.clip(jax.random.normal(key, (order, order), jnp.float32), -3.0, 3.0)
    mixed = (entries + entries.T) * 0.7071
    outer_scale = scale_vector[:, None] * scale_vector[None, :]
    values = outer_scale * (0.6 + 0.3 * mixed) + jnp.eye(order, dtype=jnp.float32) * outer_scale
    return values.astype(jnp.float32)


def draw_factor_a(key, part):
    input_scale, output_scale = channel_scales(key)
    return symmetric_factor(jax.random.fold_in(key, 41), input_scale, CIN)


def draw_factor_g(key, part):
    input_scale, output_scale = channel_scales(key)
    return symmetric_factor(jax.random.fold_in(key, 51), output_scale, COUT)


def shard_levels(stream_key, extent, pieces, smallest, largest):
    factor_of = 1.0
    for position, blocks in pieces:
        steps = jax.random.uniform(jax.random.fold_in(jax.random.fold_in(stream_key, 6), position), (blocks,), jnp.float32, smallest / len(pieces), largest / len(pieces))
        factor_of = factor_of * jnp.repeat(jnp.exp(steps), extent[position] // blocks).reshape((-1,) + (1,) * (len(extent) - 1 - position))
    return factor_of


def scatter_about(key, dims, width, limit, shards=(), kind=jnp.bfloat16):
    gain = shard_levels(key, dims, shards, -0.22, 0.18) if shards else 1.0
    values = jax.random.normal(key, dims, jnp.float32) * width * gain
    return jnp.minimum(jnp.maximum(values, -limit), limit).astype(kind)


def setup_inputs(seed: int = 0) -> dict:
    key_list = jax.random.split(jax.random.key(seed), 7)
    activations = draw_activations(jax.random.fold_in(key_list[6], 71), 0)
    out_grads = draw_out_grads(jax.random.fold_in(key_list[6], 71), 0)
    factor_a = draw_factor_a(jax.random.fold_in(key_list[6], 71), 0)
    factor_g = draw_factor_g(jax.random.fold_in(key_list[6], 71), 0)
    inverse_a = scatter_about(key_list[4], (CIN, CIN), CIN ** -0.5, 0.1875, ((0, 8),), jnp.float32)
    inverse_g = scatter_about(key_list[5], (COUT, COUT), COUT ** -0.5, 0.375, ((0, 8),), jnp.float32)
    return dict(activations=activations, out_grads=out_grads, factor_a=factor_a, factor_g=factor_g, inverse_a=inverse_a, inverse_g=inverse_g)


decay_rate = 0.6


def reference(activations, out_grads, factor_a, factor_g, inverse_a, inverse_g):
    highest = lax.Precision.HIGHEST
    contract = (((0,), (0,)), ((), ()))
    stat_a = lax.dot_general(activations, activations, contract, precision=highest, preferred_element_type=jnp.float32) / ROWS
    stat_g = lax.dot_general(out_grads, out_grads, contract, precision=highest, preferred_element_type=jnp.float32)
    grad = lax.dot_general(activations, out_grads, contract, precision=highest, preferred_element_type=jnp.float32)
    new_factor_a = decay_rate * factor_a + (1.0 - decay_rate) * stat_a
    new_factor_g = decay_rate * factor_g + (1.0 - decay_rate) * stat_g
    right = jnp.dot(grad, inverse_g, precision=highest, preferred_element_type=jnp.float32)
    precond_grad = jnp.dot(inverse_a, right, precision=highest, preferred_element_type=jnp.float32)
    return new_factor_a, new_factor_g, precond_grad
```

```python
import functools

import jax
import jax.numpy as jnp
from jax import lax
from jax.experimental import pallas as pl
from jax.experimental.pallas import tpu as pltpu
from jax.sharding import PartitionSpec as P

decay_rate = 0.6
MESH = pl.DeviceIdType.MESH
BF = jnp.bfloat16
F32 = jnp.float32
LOAD_ROWS = 256
LOAD_SLOTS = 4
TILE = 512


def split(x):
    hi = x.astype(BF)
    return hi, (x - hi.astype(F32)).astype(BF)


def mm(a, b):
    return jnp.dot(a, b, preferred_element_type=F32)


def mm3(a_hi, a_lo, b_hi, b_lo):
    return mm(a_hi, b_hi) + (mm(a_hi, b_lo) + mm(a_lo, b_hi))


def step_kernel(
    dims, a_hbm, g_hbm, ia_ref, ig_ref, out_a, out_g, out_p,
    a_buf, g_buf, hi, lo, hi_t, lo_t, ig_full, right, *rest,
):
    n_panel, n_rep, rows, cin, cout, chunk_rows = dims
    chunks = len(chunk_rows)
    sums, landed, z_landed, final = (rest[i * chunks : (i + 1) * chunks] for i in range(4))
    (a_sem, g_sem, ig_send, ig_recv, own_sem, h_send, h_recv, z_send, z_recv, f_send, f_recv, r_send, r_recv) = rest[4 * chunks :]
    own, own_g = cin // n_panel, cout // n_panel
    half = cout // 2
    levels = n_panel.bit_length() - 1
    me = lax.axis_index("panel")
    rep = lax.axis_index("rep")

    blocks = rows // LOAD_ROWS

    def a_load(block, slot):
        return pltpu.make_async_copy(
            a_hbm.at[pl.ds(pl.multiple_of(block * LOAD_ROWS, LOAD_ROWS), LOAD_ROWS)], a_buf.at[slot], a_sem.at[slot]
        )

    def g_load(block, slot):
        return pltpu.make_async_copy(
            g_hbm.at[pl.ds(pl.multiple_of(block * LOAD_ROWS, LOAD_ROWS), LOAD_ROWS)], g_buf.at[slot], g_sem.at[slot]
        )

    for block in range(LOAD_SLOTS):
        a_load(block, block).start()
        g_load(block, block).start()

    barrier = pltpu.get_barrier_semaphore()
    for k in range(1, n_panel):
        pl.semaphore_signal(barrier, inc=1, device_id={"panel": me ^ k}, device_id_type=MESH)
    for k in range(1, n_rep):
        pl.semaphore_signal(barrier, inc=1, device_id={"rep": lax.rem(rep + k, n_rep)}, device_id_type=MESH)

    def prepare(block, carry):
        slot = lax.rem(block, LOAD_SLOTS)
        a_load(block, slot).wait()
        g_load(block, slot).wait()
        at = pl.ds(pl.multiple_of(block * LOAD_ROWS, LOAD_ROWS), LOAD_ROWS)
        for piece in range(cin // cout + 1):
            cols = pl.ds(piece * cout, cout)
            x = a_buf[slot, :, cols] if piece < cin // cout else g_buf[slot]
            h, l = split(x)
            hi[at, cols] = h
            lo[at, cols] = l
            h, l = split(x.T)
            hi_t[cols, at] = h
            lo_t[cols, at] = l

        @pl.when(block + LOAD_SLOTS < blocks)
        def _():
            a_load(block + LOAD_SLOTS, slot).start()
            g_load(block + LOAD_SLOTS, slot).start()

        return carry

    lax.fori_loop(0, blocks, prepare, 0)

    pl.semaphore_wait(barrier, n_panel - 1 + n_rep - 1)

    own_copy = pltpu.make_async_copy(ig_ref, ig_full.at[me], own_sem)
    own_copy.start()

    def ig_copy(k):
        return pltpu.make_async_remote_copy(
            ig_ref, ig_full.at[me], ig_send.at[k], ig_recv.at[k], device_id={"panel": me ^ k}, device_id_type=MESH
        )

    for k in range(1, n_panel):
        ig_copy(k).start()

    orders = ([*range(levels)], [0, *reversed(range(1, levels))])

    def slot_of(h, panel):
        slot = 0
        for level, bit in enumerate(orders[h]):
            slot = slot + (((panel >> bit) & 1) << (levels - 1 - level))
        return slot

    def kept(h, level):
        base = 0
        for l in range(level):
            base = base + (((me >> orders[h][l]) & 1) << (levels - 1 - l))
        return base

    def multiply(c, tile):
        first = tile * TILE
        tall = min(TILE, cin + (cout if c == 0 else 0) - first)
        cols = pl.ds(cin if c == 0 else (c - 1) * cout, cout)
        m = pl.ds(first, tall)
        out = mm3(hi_t[m, :], lo_t[m, :], hi[:, cols], lo[:, cols])
        for h in range(2):
            part = out[:, h * half : (h + 1) * half]
            if first < cin:
                for j in range(tall // own):
                    sums[c][h, slot_of(h, first // own + j), :own] = part[j * own : (j + 1) * own]
            else:
                for j in range(n_panel):
                    sums[c][h, slot_of(h, j), pl.ds(own, own_g)] = part[j * own_g : (j + 1) * own_g]
                    if chunk_rows[0] > own + own_g:
                        pad = chunk_rows[0] - own - own_g
                        sums[c][h, slot_of(h, j), pl.ds(own + own_g, pad)] = jnp.zeros((pad, half), F32)

    def halving(c, h, level):
        size = 1 << (levels - 1 - level)
        bit = orders[h][level]
        away = kept(h, level) + (1 - ((me >> bit) & 1)) * size
        return pltpu.make_async_remote_copy(
            sums[c].at[h, pl.ds(away, size)],
            landed[c].at[h, pl.ds(n_panel - 2 * size, size)],
            h_send.at[c, h, level],
            h_recv.at[c, h, level],
            device_id={"panel": me ^ (1 << bit)},
            device_id_type=MESH,
        )

    def add_half(c, h, level):
        size = 1 << (levels - 1 - level)
        at = pl.ds(kept(h, level + 1), size)
        sums[c][h, at] = sums[c][h, at] + landed[c][h, pl.ds(n_panel - 2 * size, size)]

    def part_rows(c, owner):
        tall = chunk_rows[c] // n_rep
        return pl.ds(pl.multiple_of(owner * tall, tall), tall)

    def z_scatter(c, h, k):
        to = lax.rem(rep + k, n_rep)
        return pltpu.make_async_remote_copy(
            sums[c].at[h, slot_of(h, me), part_rows(c, to)],
            z_landed[c].at[k, h],
            z_send.at[c, h, k],
            z_recv.at[c, h, k],
            device_id={"rep": to},
            device_id_type=MESH,
        )

    def z_gather(c, h, k):
        at = part_rows(c, rep)
        return pltpu.make_async_remote_copy(
            final[c].at[h, at],
            final[c].at[h, at],
            f_send.at[c, h, k],
            f_recv.at[c, h, k],
            device_id={"rep": lax.rem(rep + k, n_rep)},
            device_id_type=MESH,
        )

    def right_copy(level, m):
        bit = levels - 1 - level
        return pltpu.make_async_remote_copy(
            right.at[me ^ m],
            right.at[me ^ m],
            r_send.at[level, m >> (bit + 1)],
            r_recv.at[level, m >> (bit + 1)],
            device_id={"panel": me ^ (1 << bit)},
            device_id_type=MESH,
        )

    def right_level(level):
        bit = levels - 1 - level
        return [right_copy(level, m << (bit + 1)) for m in range(1 << level)]

    def stage(c, s):
        if s > 0 and s <= levels:
            for h in range(2):
                halving(c, h, s - 1).wait()
                add_half(c, h, s - 1)
                if s < levels:
                    halving(c, h, s).start()
                else:
                    for k in range(1, n_rep):
                        z_scatter(c, h, k).start()
        elif s == 0:
            for h in range(2):
                halving(c, h, 0).start()
        elif s == levels + 1:
            for h in range(2):
                at = part_rows(c, rep)
                total = sums[c][h, slot_of(h, me), at]
                for k in range(1, n_rep):
                    z_scatter(c, h, k).wait()
                    total = total + z_landed[c][k, h]
                final[c][h, at] = total
                for k in range(1, n_rep):
                    z_gather(c, h, k).start()
        elif s == levels + 2:
            for h in range(2):
                for k in range(1, n_rep):
                    z_gather(c, h, k).wait()
            if c > 0:
                for h in range(2):
                    out_a[:, pl.ds((c - 1) * cout + h * half, half)] = final[c][h, :own]
            else:
                own_copy.wait()
                for k in range(1, n_panel):
                    ig_copy(k).wait()
                ig_hi, ig_lo = split(ig_full[...].reshape(cout, cout))
                acc = jnp.zeros((own, cout), F32)
                for h in range(2):
                    out_g[:, pl.ds(h * half, half)] = final[0][h, pl.ds(own, own_g)]
                    g_hi, g_lo = split(final[0][h, :own])
                    at = slice(h * half, (h + 1) * half)
                    acc = acc + mm3(g_hi, g_lo, ig_hi[at], ig_lo[at])
                right[me] = acc
                for copy in right_level(0):
                    copy.start()
        else:
            level = s - levels - 3
            for copy in right_level(level):
                copy.wait()
            if level + 1 < levels:
                for copy in right_level(level + 1):
                    copy.start()
            else:
                r_hi, r_lo = split(right[...].reshape(cin, cout))
                i_hi, i_lo = split(ia_ref[...])
                out_p[...] = mm3(i_hi, i_lo, r_hi, r_lo)

    waiting = []
    for c in range(chunks):
        tall = cin + (cout if c == 0 else 0)
        tiles = -(-tall // TILE)
        for tile in range(tiles):
            multiply(c, tile)
            if tile == tiles - 1:
                waiting.append([c, 0])
            for item in waiting:
                if item[1] < levels + 3 + (levels if item[0] == 0 else 0):
                    stage(*item)
                    item[1] += 1
    while any(s < levels + 3 + (levels if c == 0 else 0) for c, s in waiting):
        for item in waiting:
            if item[1] < levels + 3 + (levels if item[0] == 0 else 0):
                stage(*item)
                item[1] += 1


def local(activations, out_grads, factor_a, factor_g, inverse_a, inverse_g):
    n_panel, n_rep = lax.axis_size("panel"), lax.axis_size("rep")
    rows, cin = activations.shape
    cout = out_grads.shape[1]
    total_rows = rows * n_panel * n_rep
    own, own_g = cin // n_panel, cout // n_panel
    unit = 8 * n_rep
    chunks = cin // cout + 1
    chunk_rows = (-(-(own + own_g) // unit) * unit,) + (own,) * (chunks - 1)
    levels = n_panel.bit_length() - 1
    half = cout // 2
    dma = pltpu.SemaphoreType.DMA
    dims = (n_panel, n_rep, rows, cin, cout, chunk_rows)
    vmem = pl.BlockSpec(memory_space=pltpu.VMEM)
    hbm = pl.BlockSpec(memory_space=pl.ANY)
    joint, small, precond_grad = pl.pallas_call(
        functools.partial(step_kernel, dims),
        out_shape=(
            jax.ShapeDtypeStruct((own, cin), F32),
            jax.ShapeDtypeStruct((own_g, cout), F32),
            jax.ShapeDtypeStruct((own, cout), F32),
        ),
        in_specs=[hbm, hbm, vmem, vmem],
        out_specs=(vmem, vmem, vmem),
        scratch_shapes=[
            pltpu.VMEM((LOAD_SLOTS, LOAD_ROWS, cin), F32),
            pltpu.VMEM((LOAD_SLOTS, LOAD_ROWS, cout), F32),
            pltpu.VMEM((rows, cin + cout), BF),
            pltpu.VMEM((rows, cin + cout), BF),
            pltpu.VMEM((cin + cout, rows), BF),
            pltpu.VMEM((cin + cout, rows), BF),
            pltpu.VMEM((n_panel, own_g, cout), F32),
            pltpu.VMEM((n_panel, own, cout), F32),
            *[pltpu.VMEM((2, n_panel, r, half), F32) for r in chunk_rows],
            *[pltpu.VMEM((2, n_panel - 1, r, half), F32) for r in chunk_rows],
            *[pltpu.VMEM((n_rep, 2, r // n_rep, half), F32) for r in chunk_rows],
            *[pltpu.VMEM((2, r, half), F32) for r in chunk_rows],
            dma((LOAD_SLOTS,)),
            dma((LOAD_SLOTS,)),
            dma((n_panel,)),
            dma((n_panel,)),
            dma,
            dma((chunks, 2, levels)),
            dma((chunks, 2, levels)),
            dma((chunks, 2, n_rep)),
            dma((chunks, 2, n_rep)),
            dma((chunks, 2, n_rep)),
            dma((chunks, 2, n_rep)),
            dma((levels, n_panel // 2)),
            dma((levels, n_panel // 2)),
        ],
        compiler_params=pltpu.CompilerParams(
            collective_id=0, has_side_effects=True, vmem_limit_bytes=67043328
        ),
    )(activations, out_grads, inverse_a, inverse_g)
    new_factor_a = decay_rate * factor_a + (1.0 - decay_rate) * (joint / total_rows)
    new_factor_g = decay_rate * factor_g + (1.0 - decay_rate) * small
    return (new_factor_a, new_factor_g, precond_grad)


def solution(mesh):
    in_specs = (
        P(("panel", "rep"), None),
        P(("panel", "rep"), None),
        P("panel", None),
        P("panel", None),
        P("panel", None),
        P("panel", None),
    )
    out_specs = (P("panel", None), P("panel", None), P("panel", None))
    return jax.shard_map(local, mesh=mesh, in_specs=in_specs, out_specs=out_specs, check_vma=False)
```

```python
import functools

import jax
import jax.numpy as jnp
from jax import lax
from jax.experimental import pallas as pl
from jax.experimental.pallas import tpu as pltpu
from jax.sharding import PartitionSpec as P

decay_rate = 0.6
MESH = pl.DeviceIdType.MESH
BF = jnp.bfloat16
F32 = jnp.float32
LOAD_ROWS = 256
LOAD_SLOTS = 4
TILE = 512


def split(x):
    hi = x.astype(BF)
    return hi, (x - hi.astype(F32)).astype(BF)


def mm(a, b):
    return jnp.dot(a, b, preferred_element_type=F32)


def mm3(a_hi, a_lo, b_hi, b_lo):
    return mm(a_hi, b_hi) + (mm(a_hi, b_lo) + mm(a_lo, b_hi))


def step_kernel(
    dims, a_hbm, g_hbm, ia_ref, ig_ref, out_a, out_g, out_p,
    a_buf, g_buf, hi, lo, hi_t, lo_t, ig_full, right, *rest,
):
    n_panel, n_rep, rows, cin, cout, chunk_rows = dims
    chunks = len(chunk_rows)
    sums, landed, z_landed, final = (rest[i * chunks : (i + 1) * chunks] for i in range(4))
    (a_sem, g_sem, ig_send, ig_recv, own_sem, h_send, h_recv, z_send, z_recv, f_send, f_recv, r_send, r_recv) = rest[4 * chunks :]
    own, own_g = cin // n_panel, cout // n_panel
    half = cout // 2
    levels, z_levels = n_panel.bit_length() - 1, n_rep.bit_length() - 1
    last = levels + 2 * z_levels
    me = lax.axis_index("panel")
    rep = lax.axis_index("rep")

    orders = ([*range(levels)], [0, *reversed(range(1, levels))])

    def slot_of(h, panel):
        slot = 0
        for level, bit in enumerate(orders[h]):
            slot = slot + (((panel >> bit) & 1) << (levels - 1 - level))
        return slot

    blocks = rows // LOAD_ROWS

    def a_load(block, slot):
        return pltpu.make_async_copy(
            a_hbm.at[pl.ds(pl.multiple_of(block * LOAD_ROWS, LOAD_ROWS), LOAD_ROWS)], a_buf.at[slot], a_sem.at[slot]
        )

    def g_load(block, slot):
        return pltpu.make_async_copy(
            g_hbm.at[pl.ds(pl.multiple_of(block * LOAD_ROWS, LOAD_ROWS), LOAD_ROWS)], g_buf.at[slot], g_sem.at[slot]
        )

    for block in range(LOAD_SLOTS):
        a_load(block, block).start()
        g_load(block, block).start()

    barrier = pltpu.get_barrier_semaphore()
    for k in range(1, n_panel):
        pl.semaphore_signal(barrier, inc=1, device_id={"panel": me ^ k}, device_id_type=MESH)
    for level in range(z_levels):
        pl.semaphore_signal(barrier, inc=1, device_id={"rep": rep ^ (1 << level)}, device_id_type=MESH)

    def prepare(block, carry):
        slot = lax.rem(block, LOAD_SLOTS)
        a_load(block, slot).wait()
        g_load(block, slot).wait()
        at = pl.ds(pl.multiple_of(block * LOAD_ROWS, LOAD_ROWS), LOAD_ROWS)
        g_hi, g_lo = split(g_buf[slot])
        for piece in range(cin // cout + 1):
            cols = pl.ds(piece * cout, cout)
            if piece < cin // cout:
                x = a_buf[slot, :, cols]
                h, l = split(x)
                hi[at, cols] = h
                lo[at, cols] = l
                h, l = split(x.T)
                hi_t[cols, at] = h
                lo_t[cols, at] = l
                tall, offset = own, 0
            else:
                h, l = split(g_buf[slot].T)
                tall, offset = own_g, own
            out = mm3(h, l, g_hi, g_lo)
            for j in range(cout // tall):
                panel = j if offset else piece * (cout // own) + j
                for side in range(2):
                    dst = sums[0].at[side, slot_of(side, panel), pl.ds(offset, tall)]
                    dst[...] = dst[...] + out[j * tall : (j + 1) * tall, side * half : (side + 1) * half]

        @pl.when(block + LOAD_SLOTS < blocks)
        def _():
            a_load(block + LOAD_SLOTS, slot).start()
            g_load(block + LOAD_SLOTS, slot).start()

        return carry

    sums[0][...] = jnp.zeros_like(sums[0])
    lax.fori_loop(0, blocks, prepare, 0)

    pl.semaphore_wait(barrier, n_panel - 1 + z_levels)

    own_copy = pltpu.make_async_copy(ig_ref, ig_full.at[me], own_sem)
    own_copy.start()

    def ig_copy(k):
        return pltpu.make_async_remote_copy(
            ig_ref, ig_full.at[me], ig_send.at[k], ig_recv.at[k], device_id={"panel": me ^ k}, device_id_type=MESH
        )

    for k in range(1, n_panel):
        ig_copy(k).start()

    def kept(h, level):
        base = 0
        for l in range(level):
            base = base + (((me >> orders[h][l]) & 1) << (levels - 1 - l))
        return base

    def multiply(c, tile):
        first = tile * TILE
        m, cols = pl.ds(first, TILE), pl.ds((c - 1) * cout, cout)
        out = mm3(hi_t[m, :], lo_t[m, :], hi[:, cols], lo[:, cols])
        for h in range(2):
            for j in range(TILE // own):
                sums[c][h, slot_of(h, first // own + j)] = out[j * own : (j + 1) * own, h * half : (h + 1) * half]

    def halving(c, h, level):
        size = 1 << (levels - 1 - level)
        bit = orders[h][level]
        away = kept(h, level) + (1 - ((me >> bit) & 1)) * size
        return pltpu.make_async_remote_copy(
            sums[c].at[h, pl.ds(away, size)],
            landed[c].at[h, pl.ds(n_panel - 2 * size, size)],
            h_send.at[c, h, level],
            h_recv.at[c, h, level],
            device_id={"panel": me ^ (1 << bit)},
            device_id_type=MESH,
        )

    def add_half(c, h, level):
        size = 1 << (levels - 1 - level)
        at = pl.ds(kept(h, level + 1), size)
        sums[c][h, at] = sums[c][h, at] + landed[c][h, pl.ds(n_panel - 2 * size, size)]

    def z_base(c, level):
        base = 0
        for l in range(level):
            base = base + ((rep >> l) & 1) * (chunk_rows[c] >> (l + 1))
        return base

    def z_rows(c, base, tall):
        return pl.ds(pl.multiple_of(base, chunk_rows[c] // n_rep), tall)

    def z_scatter(c, h, level):
        tall = chunk_rows[c] >> (level + 1)
        away = z_base(c, level) + (1 - ((rep >> level) & 1)) * tall
        return pltpu.make_async_remote_copy(
            sums[c].at[h, slot_of(h, me), z_rows(c, away, tall)],
            z_landed[c].at[h, pl.ds(chunk_rows[c] - 2 * tall, tall)],
            z_send.at[c, h, level],
            z_recv.at[c, h, level],
            device_id={"rep": rep ^ (1 << level)},
            device_id_type=MESH,
        )

    def z_add(c, h, level):
        tall = chunk_rows[c] >> (level + 1)
        at = z_rows(c, z_base(c, level + 1), tall)
        total = sums[c][h, slot_of(h, me), at] + z_landed[c][h, pl.ds(chunk_rows[c] - 2 * tall, tall)]
        if level + 1 < z_levels:
            sums[c][h, slot_of(h, me), at] = total
        else:
            final[c][h, at] = total

    def z_gather(c, h, level):
        at = z_rows(c, z_base(c, level + 1), chunk_rows[c] >> (level + 1))
        return pltpu.make_async_remote_copy(
            final[c].at[h, at],
            final[c].at[h, at],
            f_send.at[c, h, level],
            f_recv.at[c, h, level],
            device_id={"rep": rep ^ (1 << level)},
            device_id_type=MESH,
        )

    def right_copy(level, m):
        bit = levels - 1 - level
        return pltpu.make_async_remote_copy(
            right.at[me ^ m],
            right.at[me ^ m],
            r_send.at[level, m >> (bit + 1)],
            r_recv.at[level, m >> (bit + 1)],
            device_id={"panel": me ^ (1 << bit)},
            device_id_type=MESH,
        )

    def right_level(level):
        bit = levels - 1 - level
        return [right_copy(level, m << (bit + 1)) for m in range(1 << level)]

    def stage(c, s):
        if s < last:
            for h in range(2):
                if 0 < s <= levels:
                    halving(c, h, s - 1).wait()
                    add_half(c, h, s - 1)
                elif levels < s <= levels + z_levels:
                    z_scatter(c, h, s - levels - 1).wait()
                    z_add(c, h, s - levels - 1)
                elif s > levels + z_levels:
                    z_gather(c, h, last - s).wait()
                if s < levels:
                    halving(c, h, s).start()
                elif s < levels + z_levels:
                    z_scatter(c, h, s - levels).start()
                else:
                    z_gather(c, h, last - 1 - s).start()
        elif s == last:
            for h in range(2):
                z_gather(c, h, 0).wait()
            if c > 0:
                for h in range(2):
                    out_a[:, pl.ds((c - 1) * cout + h * half, half)] = final[c][h, :own]
            else:
                own_copy.wait()
                for k in range(1, n_panel):
                    ig_copy(k).wait()
                ig_hi, ig_lo = split(ig_full[...].reshape(cout, cout))
                acc = jnp.zeros((own, cout), F32)
                for h in range(2):
                    out_g[:, pl.ds(h * half, half)] = final[0][h, pl.ds(own, own_g)]
                    g_hi, g_lo = split(final[0][h, :own])
                    at = slice(h * half, (h + 1) * half)
                    acc = acc + mm3(g_hi, g_lo, ig_hi[at], ig_lo[at])
                right[me] = acc
                for copy in right_level(0):
                    copy.start()
        else:
            level = s - last - 1
            for copy in right_level(level):
                copy.wait()
            if level + 1 < levels:
                for copy in right_level(level + 1):
                    copy.start()
            else:
                r_hi, r_lo = split(right[...].reshape(cin, cout))
                i_hi, i_lo = split(ia_ref[...])
                out_p[...] = mm3(i_hi, i_lo, r_hi, r_lo)

    def cost(c, s):
        if s == 0:
            return "core", 1.6, 1.0
        if s < levels:
            return "xy", (2.8, 1.4)[min(s - 1, 1)], 1.6
        if s < last:
            return "z", 1.4, 1.9
        return "xy", (1.4, 2.8, 1.6)[min(s - last, 2)], 1.6

    tiles = [(c, tile) for c in range(1, chunks) for tile in range(cin // TILE)]
    ends = {c: last + (levels if c == 0 else 0) for c in range(chunks)}
    ready, free, now = {(0, 0): 0.0}, {}, 0.0
    while ready or tiles:
        due = [item for item in ready if ready[item] <= now]
        if not due and tiles:
            c, tile = tiles.pop(0)
            multiply(c, tile)
            now += 1.8
            if tile == cin // TILE - 1:
                ready[c, 0] = now
            continue
        c, s = min(due) if due else min(ready, key=lambda item: (ready[item], item))
        now = max(now, ready.pop((c, s))) + 0.2
        stage(c, s)
        if s < ends[c]:
            link, busy, lag = cost(c, s)
            free[link] = max(free.get(link, 0.0), now) + busy
            ready[c, s + 1] = free[link] + lag


def local(activations, out_grads, factor_a, factor_g, inverse_a, inverse_g):
    n_panel, n_rep = lax.axis_size("panel"), lax.axis_size("rep")
    rows, cin = activations.shape
    cout = out_grads.shape[1]
    total_rows = rows * n_panel * n_rep
    own, own_g = cin // n_panel, cout // n_panel
    unit = 8 * n_rep
    chunks = cin // cout + 1
    chunk_rows = (-(-(own + own_g) // unit) * unit,) + (own,) * (chunks - 1)
    levels = n_panel.bit_length() - 1
    half = cout // 2
    dma = pltpu.SemaphoreType.DMA
    dims = (n_panel, n_rep, rows, cin, cout, chunk_rows)
    vmem = pl.BlockSpec(memory_space=pltpu.VMEM)
    hbm = pl.BlockSpec(memory_space=pl.ANY)
    joint, small, precond_grad = pl.pallas_call(
        functools.partial(step_kernel, dims),
        out_shape=(
            jax.ShapeDtypeStruct((own, cin), F32),
            jax.ShapeDtypeStruct((own_g, cout), F32),
            jax.ShapeDtypeStruct((own, cout), F32),
        ),
        in_specs=[hbm, hbm, vmem, vmem],
        out_specs=(vmem, vmem, vmem),
        scratch_shapes=[
            pltpu.VMEM((LOAD_SLOTS, LOAD_ROWS, cin), F32),
            pltpu.VMEM((LOAD_SLOTS, LOAD_ROWS, cout), F32),
            pltpu.VMEM((rows, cin), BF),
            pltpu.VMEM((rows, cin), BF),
            pltpu.VMEM((cin, rows), BF),
            pltpu.VMEM((cin, rows), BF),
            pltpu.VMEM((n_panel, own_g, cout), F32),
            pltpu.VMEM((n_panel, own, cout), F32),
            *[pltpu.VMEM((2, n_panel, r, half), F32) for r in chunk_rows],
            *[pltpu.VMEM((2, n_panel - 1, r, half), F32) for r in chunk_rows],
            *[pltpu.VMEM((2, r, half), F32) for r in chunk_rows],
            *[pltpu.VMEM((2, r, half), F32) for r in chunk_rows],
            dma((LOAD_SLOTS,)),
            dma((LOAD_SLOTS,)),
            dma((n_panel,)),
            dma((n_panel,)),
            dma,
            dma((chunks, 2, levels)),
            dma((chunks, 2, levels)),
            dma((chunks, 2, n_rep)),
            dma((chunks, 2, n_rep)),
            dma((chunks, 2, n_rep)),
            dma((chunks, 2, n_rep)),
            dma((levels, n_panel // 2)),
            dma((levels, n_panel // 2)),
        ],
        compiler_params=pltpu.CompilerParams(
            collective_id=0, has_side_effects=True, vmem_limit_bytes=67043328
        ),
    )(activations, out_grads, inverse_a, inverse_g)
    new_factor_a = decay_rate * factor_a + (1.0 - decay_rate) * (joint / total_rows)
    new_factor_g = decay_rate * factor_g + (1.0 - decay_rate) * small
    return (new_factor_a, new_factor_g, precond_grad)


def solution(mesh):
    in_specs = (
        P(("panel", "rep"), None),
        P(("panel", "rep"), None),
        P("panel", None),
        P("panel", None),
        P("panel", None),
        P("panel", None),
    )
    out_specs = (P("panel", None), P("panel", None), P("panel", None))
    return jax.shard_map(local, mesh=mesh, in_specs=in_specs, out_specs=out_specs, check_vma=False)
```

```python
import functools

import jax
import jax.numpy as jnp
from jax import lax
from jax.experimental import pallas as pl
from jax.experimental.pallas import tpu as pltpu
from jax.sharding import PartitionSpec as P

decay_rate = 0.6
MESH = pl.DeviceIdType.MESH
BF = jnp.bfloat16
F32 = jnp.float32
LOAD_ROWS = 256
LOAD_SLOTS = 4
TILE = 512
SLACK = 1.0


def split(x):
    hi = x.astype(BF)
    return hi, (x - hi.astype(F32)).astype(BF)


def mm(a, b):
    return jnp.dot(a, b, preferred_element_type=F32)


def mm3(a_hi, a_lo, b_hi, b_lo):
    return mm(a_hi, b_hi) + (mm(a_hi, b_lo) + mm(a_lo, b_hi))


def step_kernel(
    dims, a_hbm, g_hbm, ia_ref, ig_ref, out_a, out_g, out_p,
    a_buf, g_buf, hi, lo, hi_t, lo_t, ig_full, right, *rest,
):
    n_panel, n_rep, rows, cin, cout, chunk_rows = dims
    chunks = len(chunk_rows)
    sums, landed, z_landed, final = (rest[i * chunks : (i + 1) * chunks] for i in range(4))
    (a_sem, g_sem, ig_send, ig_recv, own_sem, h_send, h_recv, z_send, z_recv, f_send, f_recv, r_send, r_recv) = rest[4 * chunks :]
    own, own_g = cin // n_panel, cout // n_panel
    half = cout // 2
    levels, z_levels = n_panel.bit_length() - 1, n_rep.bit_length() - 1
    last = levels + 2 * z_levels
    me = lax.axis_index("panel")
    rep = lax.axis_index("rep")

    orders = ([*range(levels)], [0, *reversed(range(1, levels))])

    def slot_of(h, panel):
        slot = 0
        for level, bit in enumerate(orders[h]):
            slot = slot + (((panel >> bit) & 1) << (levels - 1 - level))
        return slot

    blocks = rows // LOAD_ROWS

    def a_load(block, slot):
        return pltpu.make_async_copy(
            a_hbm.at[pl.ds(pl.multiple_of(block * LOAD_ROWS, LOAD_ROWS), LOAD_ROWS)], a_buf.at[slot], a_sem.at[slot]
        )

    def g_load(block, slot):
        return pltpu.make_async_copy(
            g_hbm.at[pl.ds(pl.multiple_of(block * LOAD_ROWS, LOAD_ROWS), LOAD_ROWS)], g_buf.at[slot], g_sem.at[slot]
        )

    for block in range(LOAD_SLOTS):
        a_load(block, block).start()
        g_load(block, block).start()

    barrier = pltpu.get_barrier_semaphore()
    for k in range(1, n_panel):
        pl.semaphore_signal(barrier, inc=1, device_id={"panel": me ^ k}, device_id_type=MESH)
    for level in range(z_levels):
        pl.semaphore_signal(barrier, inc=1, device_id={"rep": rep ^ (1 << level)}, device_id_type=MESH)

    def prepare(block, carry):
        slot = lax.rem(block, LOAD_SLOTS)
        a_load(block, slot).wait()
        g_load(block, slot).wait()
        at = pl.ds(pl.multiple_of(block * LOAD_ROWS, LOAD_ROWS), LOAD_ROWS)
        g_hi, g_lo = split(g_buf[slot])
        for piece in range(cin // cout + 1):
            cols = pl.ds(piece * cout, cout)
            if piece < cin // cout:
                x = a_buf[slot, :, cols]
                h, l = split(x)
                hi[at, cols] = h
                lo[at, cols] = l
                h, l = split(x.T)
                hi_t[cols, at] = h
                lo_t[cols, at] = l
                tall, offset = own, 0
            else:
                h, l = split(g_buf[slot].T)
                tall, offset = own_g, own
            out = mm3(h, l, g_hi, g_lo)
            for j in range(cout // tall):
                panel = j if offset else piece * (cout // own) + j
                for side in range(2):
                    dst = sums[0].at[side, slot_of(side, panel), pl.ds(offset, tall)]
                    dst[...] = dst[...] + out[j * tall : (j + 1) * tall, side * half : (side + 1) * half]

        @pl.when(block + LOAD_SLOTS < blocks)
        def _():
            a_load(block + LOAD_SLOTS, slot).start()
            g_load(block + LOAD_SLOTS, slot).start()

        return carry

    sums[0][...] = jnp.zeros_like(sums[0])
    lax.fori_loop(0, blocks, prepare, 0)

    pl.semaphore_wait(barrier, n_panel - 1 + z_levels)

    own_copy = pltpu.make_async_copy(ig_ref, ig_full.at[me], own_sem)
    own_copy.start()

    def ig_copy(k):
        return pltpu.make_async_remote_copy(
            ig_ref, ig_full.at[me], ig_send.at[k], ig_recv.at[k], device_id={"panel": me ^ k}, device_id_type=MESH
        )

    for k in range(1, n_panel):
        ig_copy(k).start()

    def kept(h, level):
        base = 0
        for l in range(level):
            base = base + (((me >> orders[h][l]) & 1) << (levels - 1 - l))
        return base

    def multiply(c, tile):
        first = tile * TILE
        m, cols = pl.ds(first, TILE), pl.ds((c - 1) * cout, cout)
        out = mm3(hi_t[m, :], lo_t[m, :], hi[:, cols], lo[:, cols])
        for h in range(2):
            for j in range(TILE // own):
                sums[c][h, slot_of(h, first // own + j)] = out[j * own : (j + 1) * own, h * half : (h + 1) * half]

    def halving(c, h, level):
        size = 1 << (levels - 1 - level)
        bit = orders[h][level]
        away = kept(h, level) + (1 - ((me >> bit) & 1)) * size
        return pltpu.make_async_remote_copy(
            sums[c].at[h, pl.ds(away, size)],
            landed[c].at[h, pl.ds(n_panel - 2 * size, size)],
            h_send.at[c, h, level],
            h_recv.at[c, h, level],
            device_id={"panel": me ^ (1 << bit)},
            device_id_type=MESH,
        )

    def add_half(c, h, level):
        size = 1 << (levels - 1 - level)
        at = pl.ds(kept(h, level + 1), size)
        sums[c][h, at] = sums[c][h, at] + landed[c][h, pl.ds(n_panel - 2 * size, size)]

    def z_base(c, level):
        base = 0
        for l in range(level):
            base = base + ((rep >> l) & 1) * (chunk_rows[c] >> (l + 1))
        return base

    def z_rows(c, base, tall):
        return pl.ds(pl.multiple_of(base, chunk_rows[c] // n_rep), tall)

    def z_scatter(c, h, level):
        tall = chunk_rows[c] >> (level + 1)
        away = z_base(c, level) + (1 - ((rep >> level) & 1)) * tall
        return pltpu.make_async_remote_copy(
            sums[c].at[h, slot_of(h, me), z_rows(c, away, tall)],
            z_landed[c].at[h, pl.ds(chunk_rows[c] - 2 * tall, tall)],
            z_send.at[c, h, level],
            z_recv.at[c, h, level],
            device_id={"rep": rep ^ (1 << level)},
            device_id_type=MESH,
        )

    def z_add(c, h, level):
        tall = chunk_rows[c] >> (level + 1)
        at = z_rows(c, z_base(c, level + 1), tall)
        total = sums[c][h, slot_of(h, me), at] + z_landed[c][h, pl.ds(chunk_rows[c] - 2 * tall, tall)]
        if level + 1 < z_levels:
            sums[c][h, slot_of(h, me), at] = total
        else:
            final[c][h, at] = total

    def z_gather(c, h, level):
        at = z_rows(c, z_base(c, level + 1), chunk_rows[c] >> (level + 1))
        return pltpu.make_async_remote_copy(
            final[c].at[h, at],
            final[c].at[h, at],
            f_send.at[c, h, level],
            f_recv.at[c, h, level],
            device_id={"rep": rep ^ (1 << level)},
            device_id_type=MESH,
        )

    def right_copy(level, m):
        bit = levels - 1 - level
        return pltpu.make_async_remote_copy(
            right.at[me ^ m],
            right.at[me ^ m],
            r_send.at[level, m >> (bit + 1)],
            r_recv.at[level, m >> (bit + 1)],
            device_id={"panel": me ^ (1 << bit)},
            device_id_type=MESH,
        )

    def right_level(level):
        bit = levels - 1 - level
        return [right_copy(level, m << (bit + 1)) for m in range(1 << level)]

    def stage(c, s):
        if s < last:
            for h in range(2):
                if 0 < s <= levels:
                    halving(c, h, s - 1).wait()
                    add_half(c, h, s - 1)
                elif levels < s <= levels + z_levels:
                    z_scatter(c, h, s - levels - 1).wait()
                    z_add(c, h, s - levels - 1)
                elif s > levels + z_levels:
                    z_gather(c, h, last - s).wait()
                if s < levels:
                    halving(c, h, s).start()
                elif s < levels + z_levels:
                    z_scatter(c, h, s - levels).start()
                else:
                    z_gather(c, h, last - 1 - s).start()
        elif s == last:
            for h in range(2):
                z_gather(c, h, 0).wait()
            if c > 0:
                for h in range(2):
                    out_a[:, pl.ds((c - 1) * cout + h * half, half)] = final[c][h, :own]
            else:
                own_copy.wait()
                for k in range(1, n_panel):
                    ig_copy(k).wait()
                ig_hi, ig_lo = split(ig_full[...].reshape(cout, cout))
                acc = jnp.zeros((own, cout), F32)
                for h in range(2):
                    out_g[:, pl.ds(h * half, half)] = final[0][h, pl.ds(own, own_g)]
                    g_hi, g_lo = split(final[0][h, :own])
                    at = slice(h * half, (h + 1) * half)
                    acc = acc + mm3(g_hi, g_lo, ig_hi[at], ig_lo[at])
                right[me] = acc
                for copy in right_level(0):
                    copy.start()
        else:
            level = s - last - 1
            for copy in right_level(level):
                copy.wait()
            if level + 1 < levels:
                for copy in right_level(level + 1):
                    copy.start()
            else:
                r_hi, r_lo = split(right[...].reshape(cin, cout))
                i_hi, i_lo = split(ia_ref[...])
                out_p[...] = mm3(i_hi, i_lo, r_hi, r_lo)

    def cost(c, s):
        if s == 0:
            return "core", 1.6, 1.0
        if s < levels:
            return "xy", (2.8, 1.4)[min(s - 1, 1)], 1.6
        if s < last:
            return "z", 1.4, 1.9
        return "xy", (1.4, 2.8, 1.6)[min(s - last, 2)], 1.6

    tiles = [(c, tile) for c in range(1, chunks) for tile in range(cin // TILE)]
    ends = {c: last + (levels if c == 0 else 0) for c in range(chunks)}
    ready, free, now = {(0, 0): 0.0}, {}, 0.0
    while ready or tiles:
        due = [item for item in ready if ready[item] <= now]
        if not due and tiles:
            c, tile = tiles.pop(0)
            multiply(c, tile)
            now += 1.8
            if tile == cin // TILE - 1:
                ready[c, 0] = now
            continue
        c, s = min(due) if due else min(ready, key=lambda item: (ready[item], item))
        now = max(now, ready.pop((c, s))) + 0.2
        stage(c, s)
        if s < ends[c]:
            link, busy, lag = cost(c, s)
            free[link] = max(free.get(link, 0.0), now) + busy
            ready[c, s + 1] = now + SLACK * (free[link] + lag - now)


def blend_kernel(total_rows, joint, small, precond, factor_a, factor_g, out_a, out_g, out_p):
    out_a[...] = decay_rate * factor_a[...] + (1.0 - decay_rate) * (joint[...] / total_rows)
    out_g[...] = decay_rate * factor_g[...] + (1.0 - decay_rate) * small[...]
    out_p[...] = precond[...]


def local(activations, out_grads, factor_a, factor_g, inverse_a, inverse_g):
    n_panel, n_rep = lax.axis_size("panel"), lax.axis_size("rep")
    rows, cin = activations.shape
    cout = out_grads.shape[1]
    total_rows = rows * n_panel * n_rep
    own, own_g = cin // n_panel, cout // n_panel
    unit = 8 * n_rep
    chunks = cin // cout + 1
    chunk_rows = (-(-(own + own_g) // unit) * unit,) + (own,) * (chunks - 1)
    levels = n_panel.bit_length() - 1
    half = cout // 2
    dma = pltpu.SemaphoreType.DMA
    dims = (n_panel, n_rep, rows, cin, cout, chunk_rows)
    vmem = pl.BlockSpec(memory_space=pltpu.VMEM)
    hbm = pl.BlockSpec(memory_space=pl.ANY)
    joint, small, precond_grad = pl.pallas_call(
        functools.partial(step_kernel, dims),
        out_shape=(
            jax.ShapeDtypeStruct((own, cin), F32),
            jax.ShapeDtypeStruct((own_g, cout), F32),
            jax.ShapeDtypeStruct((own, cout), F32),
        ),
        in_specs=[hbm, hbm, vmem, vmem],
        out_specs=(vmem, vmem, vmem),
        scratch_shapes=[
            pltpu.VMEM((LOAD_SLOTS, LOAD_ROWS, cin), F32),
            pltpu.VMEM((LOAD_SLOTS, LOAD_ROWS, cout), F32),
            pltpu.VMEM((rows, cin), BF),
            pltpu.VMEM((rows, cin), BF),
            pltpu.VMEM((cin, rows), BF),
            pltpu.VMEM((cin, rows), BF),
            pltpu.VMEM((n_panel, own_g, cout), F32),
            pltpu.VMEM((n_panel, own, cout), F32),
            *[pltpu.VMEM((2, n_panel, r, half), F32) for r in chunk_rows],
            *[pltpu.VMEM((2, n_panel - 1, r, half), F32) for r in chunk_rows],
            *[pltpu.VMEM((2, r, half), F32) for r in chunk_rows],
            *[pltpu.VMEM((2, r, half), F32) for r in chunk_rows],
            dma((LOAD_SLOTS,)),
            dma((LOAD_SLOTS,)),
            dma((n_panel,)),
            dma((n_panel,)),
            dma,
            dma((chunks, 2, levels)),
            dma((chunks, 2, levels)),
            dma((chunks, 2, n_rep)),
            dma((chunks, 2, n_rep)),
            dma((chunks, 2, n_rep)),
            dma((chunks, 2, n_rep)),
            dma((levels, n_panel // 2)),
            dma((levels, n_panel // 2)),
        ],
        compiler_params=pltpu.CompilerParams(
            collective_id=0, has_side_effects=True, vmem_limit_bytes=67043328
        ),
    )(activations, out_grads, inverse_a, inverse_g)
    return pl.pallas_call(
        functools.partial(blend_kernel, total_rows),
        out_shape=tuple(jax.ShapeDtypeStruct(x.shape, F32) for x in (joint, small, precond_grad)),
        in_specs=[vmem] * 5,
        out_specs=(vmem,) * 3,
    )(joint, small, precond_grad, factor_a, factor_g)


def solution(mesh):
    in_specs = (
        P(("panel", "rep"), None),
        P(("panel", "rep"), None),
        P("panel", None),
        P("panel", None),
        P("panel", None),
        P("panel", None),
    )
    out_specs = (P("panel", None), P("panel", None), P("panel", None))
    return jax.shard_map(local, mesh=mesh, in_specs=in_specs, out_specs=out_specs, check_vma=False)
```
